32 devices in a mesh: row: 4 (over y, core), col: 8 (over z, x).
Axes of the slice: x: 2, y: 2, z: 4, core: 2. Of those that a mesh axis runs over, the one named last changes fastest.
Arguments:
- feats: bfloat16 [8192, 256], P(('row', 'col')), may hold values from -6 to 6
- weight: bfloat16 [256, 256], replicated, may hold values from -0.375 to 0.375
- cotangent: bfloat16 [8192, 256], P(('row', 'col')), may hold values from -6 to 6
- tile_rows: int32 [4, 8, 80], P('row', 'col'), may hold values from 0 to 7
- tile_cols: int32 [4, 8, 80], P('row', 'col'), may hold values from 0 to 3
- counts: int32 [4, 8], P('row', 'col'), may hold values from 1 to 80, as said below
- block_values: bfloat16 [4, 8, 80, 256, 256], P('row', 'col'), may hold values from -0.078125 to 0.078125
Outputs:
- activated: bfloat16 [8192, 256], P(('row', 'col'))
- grad_feats: bfloat16 [8192, 256], P(('row', 'col'))
- grad_weight: float32 [256, 256], replicated
The draws below stay inside these ranges and needn't reach their ends.
Inputs may be any that keep to these rules, and one draw needn't show every extreme that they name: `counts`: some tile has exactly 80 live entries in every draw; list entries at or past a tile's count are ignored.
All inputs are finite; a program needn't handle non-finite values.
Results may differ from the reference program's by a relative error of at most 0.0061.
Values may be sent and summed in bfloat16 or wider, within the bound.
A program may use at most 128 MiB of HBM per device.

```python
import jax
import jax.numpy as jnp
from jax import lax

F = 256
BS = 256
BLK_DEV = 1
MAXB = 80
NODES = 8192
N_ROW = 4
N_COL = 8


def draw_counts(key, part):
    first, second, third = jax.random.split(key, 3)
    low = max(1, MAXB // 8)
    base = jax.random.randint(first, (N_ROW * N_COL,), low, MAXB // 2 + 1)
    heavy = jax.random.randint(second, (N_ROW * N_COL,), 0, 8) == 0
    chosen = jax.random.randint(third, (), 0, N_ROW * N_COL)
    places = jnp.arange(N_ROW * N_COL, dtype=jnp.int32)
    full = heavy | (places == chosen)
    return jnp.where(full, MAXB, base).astype(jnp.int32).reshape(N_ROW, N_COL)


def with_ends(values, key, least, high):
    spot = [jax.random.randint(jax.random.fold_in(key, axis), (), 0, length) for axis, length in enumerate(values.shape)]
    widest = values.shape.index(max(values.shape))
    neighbour = spot[:widest] + [(spot[widest] + 1) % values.shape[widest]] + spot[widest + 1:]
    return values.at[tuple(spot)].set(least).at[tuple(neighbour)].set(high)


def level_of(own_key, dims, cuts, low, high):
    loudness, own = 1.0, jax.random.fold_in(own_key, 6)
    for dim, blocks in cuts:
        heights = jnp.exp(jax.random.uniform(jax.random.fold_in(own, dim), (blocks,), jnp.float32, low / len(cuts), high / len(cuts)))
        loudness = loudness * jnp.repeat(heights, dims[dim] // blocks).reshape([-1 if axis == dim else 1 for axis in range(len(dims))])
    return loudness


def noise(key, dims, spread, bound, pieces=(), kind=jnp.bfloat16):
    factor_of = level_of(key, dims, pieces, -0.22, 0.18) if pieces else 1.0
    result = jax.random.normal(key, dims, jnp.float32) * spread * factor_of
    return jnp.minimum(jnp.maximum(result, -bound), bound).astype(kind)


def setup_inputs(seed: int = 0) -> dict:
    splits = jax.random.split(jax.random.key(seed), 8)
    return {
        "feats": noise(splits[0], (NODES, F), 1.0, 6.0, ((0, 32),)),
        "weight": noise(splits[1], (F, F), F ** -0.5, 0.375),
        "cotangent": noise(splits[2], (NODES, F), 1.0, 6.0, ((0, 32),)),
        "tile_rows": with_ends(jax.random.randint(splits[3], (N_ROW, N_COL, MAXB), 0, N_COL * BLK_DEV), jax.random.fold_in(splits[3], 1), 0, (N_COL * BLK_DEV) - 1).astype(jnp.int32),
        "tile_cols": with_ends(jax.random.randint(splits[4], (N_ROW, N_COL, MAXB), 0, N_ROW * BLK_DEV), jax.random.fold_in(splits[4], 1), 0, (N_ROW * BLK_DEV) - 1).astype(jnp.int32),
        "counts": draw_counts(jax.random.fold_in(splits[7], 71), 0),
        "block_values": noise(splits[6], (N_ROW, N_COL, MAXB, BS, BS), (MAXB * BS // (3 * BLK_DEV)) ** -0.5, 0.078125, ((0, 4), (1, 8))),
    }


def column_blocks(j, cols):
    return ((cols // BLK_DEV) * N_COL + j) * BLK_DEV + cols % BLK_DEV


def reference(feats, weight, cotangent, tile_rows, tile_cols, counts, block_values):
    group_blocks = N_COL * BLK_DEV
    total_blocks = NODES // BS
    flat_rows = tile_rows.reshape(-1, MAXB).astype(jnp.int32)
    flat_cols = tile_cols.reshape(-1, MAXB).astype(jnp.int32)
    flat_counts = counts.reshape(-1).astype(jnp.int32)
    flat_values = block_values.reshape(-1, MAXB, BS, BS)
    feat_blocks = feats.reshape(total_blocks, BS, F)
    slots = jnp.arange(MAXB, dtype=jnp.int32)

    def places(tile):
        i = tile // N_COL
        j = tile % N_COL
        grows = i * group_blocks + flat_rows[tile]
        gcols = column_blocks(j, flat_cols[tile])
        live = (slots < flat_counts[tile]).astype(jnp.float32)
        values = flat_values[tile].astype(jnp.float32)
        return grows, gcols, live, values

    def forward_step(total, tile):
        grows, gcols, live, values = places(tile)
        picked = feat_blocks[gcols].astype(jnp.float32)
        prods = jnp.einsum('bij,bjf->bif', values, picked) * live[:, None, None]
        return total.at[grows].add(prods), None

    tiles = jnp.arange(N_ROW * N_COL, dtype=jnp.int32)
    agg_full, _ = lax.scan(forward_step, jnp.zeros((total_blocks, BS, F), jnp.float32), tiles)
    agg = agg_full.reshape(NODES, F).astype(jnp.bfloat16)
    pre = jnp.dot(agg, weight, preferred_element_type=jnp.float32)
    sig = jax.nn.sigmoid(pre)
    activated = (pre * sig).astype(jnp.bfloat16)
    dpre = (cotangent.astype(jnp.float32) * sig * (1.0 + pre * (1.0 - sig))).astype(jnp.bfloat16)
    grad_weight = jnp.dot(agg.T, dpre, preferred_element_type=jnp.float32) * (float(NODES) ** -0.5)
    dagg = jnp.dot(dpre, weight.T, preferred_element_type=jnp.float32).astype(jnp.bfloat16)
    dagg_blocks = dagg.reshape(total_blocks, BS, F)

    def backward_step(total, tile):
        grows, gcols, live, values = places(tile)
        picked = dagg_blocks[grows].astype(jnp.float32)
        prods = jnp.einsum('bji,bjf->bif', values, picked) * live[:, None, None]
        return total.at[gcols].add(prods), None

    grad_full, _ = lax.scan(backward_step, jnp.zeros((total_blocks, BS, F), jnp.float32), tiles)
    grad_feats = grad_full.reshape(NODES, F).astype(jnp.bfloat16)
    return activated, grad_feats, grad_weight
```

```python
import functools

import jax
import jax.numpy as jnp
from jax import lax
from jax.experimental import pallas as pl
from jax.experimental.pallas import tpu as pltpu
from jax.sharding import PartitionSpec as P


def block_sums(count, values, sources, source_of, target_of, targets, dims):
    def add(e, total):
        value = lax.dynamic_index_in_dim(values, e, keepdims=False)
        source = lax.dynamic_index_in_dim(sources, source_of[e], keepdims=False)
        prod = lax.dot_general(value, source, dims, preferred_element_type=jnp.float32)
        there = lax.dynamic_index_in_dim(total, target_of[e], keepdims=False)
        return lax.dynamic_update_index_in_dim(total, there + prod, target_of[e], 0)

    start = jnp.zeros((targets, values.shape[1], sources.shape[2]), jnp.float32)
    total = lax.fori_loop(0, count, add, start)
    return total.reshape(targets * total.shape[1], total.shape[2])


def per_device(feats, weight, cotangent, tile_rows, tile_cols, counts, block_values):
    width = feats.shape[1]
    block = block_values.shape[3]
    rows_here = tile_rows[0, 0]
    cols_here = tile_cols[0, 0]
    count = counts[0, 0]
    values = block_values[0, 0]
    row_count = lax.axis_size("row")
    col_count = lax.axis_size("col")
    own_blocks = feats.shape[0] // block
    nodes = feats.shape[0] * row_count * col_count
    panel = lax.all_gather(feats, "row", axis=0, tiled=True).reshape(
        row_count * own_blocks, block, width
    )
    partial_value = block_sums(
        count, values, panel, cols_here, rows_here, col_count * own_blocks, (((1,), (0,)), ((), ()))
    )
    agg_sum = lax.psum_scatter(partial_value, "col", scatter_dimension=0, tiled=True)
    agg = agg_sum.astype(jnp.bfloat16)
    pre = jnp.dot(agg, weight, preferred_element_type=jnp.float32)
    sig = jax.nn.sigmoid(pre)
    activated = (pre * sig).astype(jnp.bfloat16)
    dpre = (cotangent.astype(jnp.float32) * sig * (1.0 + pre * (1.0 - sig))).astype(jnp.bfloat16)
    local_term = jnp.dot(agg.T, dpre, preferred_element_type=jnp.float32)
    summed_weight = lax.psum(local_term, ("row", "col"))
    grad_weight = summed_weight * float(nodes) ** (-0.5)
    dagg = jnp.dot(dpre, weight.T, preferred_element_type=jnp.float32).astype(jnp.bfloat16)
    group = lax.all_gather(dagg, "col", axis=0, tiled=True)
    group_blocks = group.reshape(col_count * own_blocks, block, width)
    back_partial = block_sums(
        count, values, group_blocks, rows_here, cols_here, row_count * own_blocks, (((0,), (0,)), ((), ()))
    )
    grad_sum = lax.psum_scatter(back_partial, "row", scatter_dimension=0, tiled=True)
    grad_feats = grad_sum.astype(jnp.bfloat16)
    return (activated, grad_feats, grad_weight)


MESH = pl.DeviceIdType.MESH
F32 = jnp.float32
BF16 = jnp.bfloat16
CHUNKS = 10
PIECES = 2


def mm(a, b):
    return jnp.dot(a, b, preferred_element_type=F32)


def densify_kernel(
    n_cols, rows_hbm, cols_hbm, counts_hbm, values, dense, held, acc, rows, cols, counts, sems
):
    most = values.shape[0]
    size = most // CHUNKS
    lists = []
    for k, (src, dst) in enumerate(((rows_hbm, rows), (cols_hbm, cols), (counts_hbm, counts))):
        lists.append(pltpu.make_async_copy(src, dst, sems.at[CHUNKS + k]))
        lists[-1].start()
    copies = []
    for k in range(CHUNKS):
        span = pl.ds(k * size, size)
        copies.append(pltpu.make_async_copy(values.at[span], held.at[span], sems.at[k]))
        copies[-1].start()

    def clear(p, carry):
        acc[p] = jnp.zeros(acc.shape[1:], F32)
        return carry

    lax.fori_loop(0, acc.shape[0], clear, 0)
    for copy in lists:
        copy.wait()
    count = counts[0, 0]

    def add(e, carry):
        place = rows[0, 0, e] * n_cols + cols[0, 0, e]
        acc[place] += held[e].astype(F32)
        return carry

    for k in range(CHUNKS):
        copies[k].wait()
        lax.fori_loop(k * size, jnp.clip(count, k * size, (k + 1) * size), add, 0)

    def settle(p, carry):
        dense[p] = acc[p].astype(BF16)
        return carry

    lax.fori_loop(0, acc.shape[0], settle, 0)


def densify(n_rows, n_cols, tile_rows, tile_cols, counts, values):
    most, block, _ = values.shape
    anywhere = pl.BlockSpec(memory_space=pltpu.HBM)
    places = n_rows * n_cols
    return pl.pallas_call(
        functools.partial(densify_kernel, n_cols),
        out_shape=jax.ShapeDtypeStruct((places, block, block), BF16),
        in_specs=[anywhere] * 4,
        out_specs=pl.BlockSpec(memory_space=pltpu.VMEM),
        scratch_shapes=[
            pltpu.VMEM((most, block, block), BF16),
            pltpu.VMEM((places, block, block), F32),
            pltpu.SMEM(tile_rows.shape, jnp.int32),
            pltpu.SMEM(tile_cols.shape, jnp.int32),
            pltpu.SMEM(counts.shape, jnp.int32),
            pltpu.SemaphoreType.DMA((CHUNKS + 3,)),
        ],
        compiler_params=pltpu.CompilerParams(vmem_limit_bytes=48 * 2**20),
        name="densify",
    )(tile_rows, tile_cols, counts, values)


def layer_kernel(
    n_row, n_col, scale, *refs
):
    panel, refs = refs[:n_row], refs[n_row:]
    (
        weight, cot, dense, act, gf, gw,
        xsend, xrecv, own, zsend, zrecv, group, back, bsend, brecv, ysend, yrecv,
        w1send, w1recv, w2, w3send, w3recv, whole, send_sems, recv_sems,
        line_send, line_recv, pair_send, pair_recv,
    ) = refs
    r = lax.axis_index("row")
    c = lax.axis_index("col")
    core = r + 1 - 2 * (r % 2)
    across = (r + 2) % n_row
    xpeer = c + 1 - 2 * (c % 2)
    x = c % 2
    z = c // 2
    n_z = n_col // 2
    started = []

    def send(src, dst, row, col):
        k = len(started)
        copy = pltpu.make_async_remote_copy(
            src_ref=src, dst_ref=dst, send_sem=send_sems.at[k], recv_sem=recv_sems.at[k],
            device_id=(row, col), device_id_type=MESH,
        )
        copy.start()
        started.append(copy)
        return copy

    barrier = pltpu.get_barrier_semaphore()
    for k in range(1, n_row):
        pl.semaphore_signal(barrier, inc=1, device_id=((r + k) % n_row, c), device_id_type=MESH)
    for k in range(1, n_col):
        pl.semaphore_signal(barrier, inc=1, device_id=(r, (c + k) % n_col), device_id_type=MESH)
    pl.semaphore_wait(barrier, n_row + n_col - 2)

    def forward(i):
        total = mm(dense[i * n_row + r], panel[0][...])
        for j in range(1, n_row):
            total += mm(dense[i * n_row + (r + n_row - j) % n_row], panel[j][...])
        return total

    partners = {3: n_z - 1 - z, 2: (z + 2) % n_z, 1: z + 1 - 2 * (z % 2), 0: z}
    cut = weight.shape[0] // PIECES
    spans = [pl.ds(h * cut, cut) for h in range(PIECES)]
    halves, arrivals = {}, {}
    for k, there in partners.items():
        xsend[k] = forward(there * 2 + 1 - x).astype(BF16)
        for h, span in enumerate(spans):
            halves[k, h] = send(xsend.at[k, span], xrecv.at[k, span], r, xpeer)
    for k, there in partners.items():
        own[k] = forward(there * 2 + x)
    for k in (3, 2, 1):
        for h, span in enumerate(spans):
            halves[k, h].wait_recv()
            zsend[k, span] = (own[k, span] + xrecv[k, span].astype(F32)).astype(BF16)
            arrivals[k, h] = send(zsend.at[k, span], zrecv.at[k, span], r, partners[k] * 2 + x)
    for h in range(PIECES):
        halves[0, h].wait_recv()
    total = own[0] + xrecv[0].astype(F32)
    for k in (3, 2, 1):
        for h in range(PIECES):
            arrivals[k, h].wait_recv()
        total += zrecv[k].astype(F32)

    agg = total.astype(BF16)
    pre = mm(agg, weight[...])
    sig = jax.nn.sigmoid(pre)
    dpre = (cot[...].astype(F32) * sig * (1.0 + pre * (1.0 - sig))).astype(BF16)
    dims = (((1,), (1,)), ((), ()))
    group[c] = lax.dot_general(weight[...], dpre, dims, preferred_element_type=F32).astype(BF16)

    def hop(way, s, h):
        source = c - 2 * s * way
        side = (1 - way) // 2
        return pltpu.make_async_remote_copy(
            src_ref=group.at[source, spans[h]], dst_ref=group.at[source, spans[h]],
            send_sem=line_send.at[side, s, h], recv_sem=line_recv.at[side, s, h],
            device_id=(r, c + 2 * way), device_id_type=MESH,
        )

    def over(way, s, h):
        source = c - 2 * s * way
        side = (1 - way) // 2
        return pltpu.make_async_remote_copy(
            src_ref=group.at[source, spans[h]], dst_ref=group.at[source, spans[h]],
            send_sem=pair_send.at[side, s, h], recv_sem=pair_recv.at[side, s, h],
            device_id=(r, xpeer), device_id_type=MESH,
        )

    def came(way, s):
        return z >= s if way == 1 else z + s < n_z

    def inner(way):
        return z < n_z - 1 if way == 1 else z > 0

    def arrived(way, s, h):
        source = c - 2 * s * way
        side = (1 - way) // 2
        return pltpu.make_async_remote_copy(
            src_ref=group.at[source, spans[h]], dst_ref=group.at[source, spans[h]],
            send_sem=line_send.at[side, s - 1, h], recv_sem=line_recv.at[side, s - 1, h],
            device_id=(r, xpeer), device_id_type=MESH,
        )

    def crossed(way, s, h):
        source = xpeer - 2 * s * way
        side = (1 - way) // 2
        return pltpu.make_async_remote_copy(
            src_ref=group.at[source, spans[h]], dst_ref=group.at[source, spans[h]],
            send_sem=pair_send.at[side, s, h], recv_sem=pair_recv.at[side, s, h],
            device_id=(r, xpeer), device_id_type=MESH,
        )

    def backward(i, first=False):
        for j in range(n_row):
            prod = mm(group[i], dense[i * n_row + j])
            back[j] = prod if first else back[j] + prod

    for h in range(PIECES):
        for way in (1, -1):

            @pl.when(inner(way))
            def _():
                hop(way, 0, h).start()

        over(1, 0, h).start()
    term = lax.dot_general(agg, dpre, (((0,), (0,)), ((), ())), preferred_element_type=F32)
    part = term.shape[0] // n_row
    for k in range(n_row):
        w1send[k] = term[k * part : (k + 1) * part].astype(BF16)
    stages = [
        [send(w1send.at[(r + k) % n_row], w1recv.at[k], (r + k) % n_row, c) for k in range(1, n_row)]
    ]
    act[...] = (pre * sig).astype(BF16)
    backward(c, True)

    def weight_sum(stage):
        for copy in stages[stage - 1]:
            copy.wait_recv()
        if stage == 1:
            total = w1send[r].astype(F32)
            for k in range(1, n_row):
                total += w1recv[k].astype(F32)
            w2[z] = total.astype(BF16)
            stages.append([send(w2.at[z], w2.at[z], r, (c + 2 * k) % n_col) for k in range(1, n_z)])
        elif stage == 2:
            total = w2[0].astype(F32)
            for k in range(1, n_z):
                total += w2[k].astype(F32)
            w3send[...] = total
            stages.append([send(w3send, w3recv, r, xpeer)])
        elif stage == 3:
            whole[r] = ((w3send[...] + w3recv[...]) * scale).astype(BF16)
            stages.append(
                [send(whole.at[r], whole.at[r], (r + k) % n_row, c) for k in range(1, n_row)]
            )

    for s in range(1, n_z):
        for h in range(PIECES):
            for way in (1, -1):

                @pl.when(came(way, s))
                def _():
                    arrived(way, s, h).wait_recv()

                    @pl.when(inner(way))
                    def _():
                        hop(way, s, h).start()

                    over(way, s, h).start()

        if s > 1:
            weight_sum(s - 1)
        for way in (1, -1):

            @pl.when(came(way, s))
            def _():
                backward(c - 2 * s * way)

    for h in range(PIECES):
        crossed(1, 0, h).wait_recv()
    backward(xpeer)
    for s in range(1, n_z):
        for way in (1, -1):

            @pl.when(came(way, s))
            def _():
                for h in range(PIECES):
                    crossed(way, s, h).wait_recv()
                backward(xpeer - 2 * s * way)

    bsend[1] = back[(core + 2) % n_row]
    second = send(bsend.at[1], brecv.at[1], core, c)
    bsend[0] = back[core]
    first = send(bsend.at[0], brecv.at[0], core, c)
    weight_sum(3)
    second.wait_recv()
    ysend[...] = (back[across] + brecv[1]).astype(BF16)
    last = send(ysend, yrecv, across, c)
    first.wait_recv()
    total = back[r] + brecv[0]
    last.wait_recv()
    total += yrecv[...].astype(F32)
    gf[...] = total.T.astype(BF16)
    weight_sum(4)
    gw[...] = whole[...].astype(F32).reshape(gw.shape)
    for copy in started:
        copy.wait_send()
    for h in range(PIECES):
        over(1, 0, h).wait_send()
        for way in (1, -1):

            @pl.when(inner(way))
            def _():
                hop(way, 0, h).wait_send()

            for s in range(1, n_z):

                @pl.when(came(way, s))
                def _():
                    over(way, s, h).wait_send()

                    @pl.when(inner(way))
                    def _():
                        hop(way, s, h).wait_send()


def finish_kernel(act, gf, gw, act_out, gf_out, gw_out, sems):
    copies = []
    for k, (src, dst) in enumerate(((act, act_out), (gf, gf_out), (gw, gw_out))):
        copies.append(pltpu.make_async_copy(src, dst, sems.at[k]))
        copies[-1].start()
    for copy in copies:
        copy.wait()


def dense_per_device(feats, weight, cotangent, tile_rows, tile_cols, counts, block_values):
    n_row = lax.axis_size("row")
    n_col = lax.axis_size("col")
    block, width = feats.shape
    dense = densify(n_col, n_row, tile_rows, tile_cols, counts, block_values[0, 0])
    scale = float(block * n_row * n_col) ** -0.5
    panel = [feats] + [
        lax.ppermute(feats, "row", [(i, (i + k) % n_row) for i in range(n_row)])
        for k in range(1, n_row)
    ]
    n_z = n_col // 2
    tile = (block, width)
    part = (width // n_row, width)
    copies = PIECES * (2 * n_z - 1) + 2 * (n_row - 1) + n_z + 3
    vmem = pl.BlockSpec(memory_space=pltpu.VMEM)
    shapes = (
        jax.ShapeDtypeStruct(tile, BF16),
        jax.ShapeDtypeStruct(tile, BF16),
        jax.ShapeDtypeStruct((width, width), F32),
    )
    results = pl.pallas_call(
        functools.partial(layer_kernel, n_row, n_col, scale),
        out_shape=shapes,
        in_specs=[vmem] * (n_row + 3),
        out_specs=(vmem, vmem, vmem),
        scratch_shapes=[
            pltpu.VMEM((n_z, *tile), BF16),
            pltpu.VMEM((n_z, *tile), BF16),
            pltpu.VMEM((n_z, *tile), F32),
            pltpu.VMEM((n_z, *tile), BF16),
            pltpu.VMEM((n_z, *tile), BF16),
            pltpu.VMEM((n_col, *tile), BF16),
            pltpu.VMEM((n_row, *tile), F32),
            pltpu.VMEM((2, *tile), F32),
            pltpu.VMEM((2, *tile), F32),
            pltpu.VMEM(tile, BF16),
            pltpu.VMEM(tile, BF16),
            pltpu.VMEM((n_row, *part), BF16),
            pltpu.VMEM((n_row, *part), BF16),
            pltpu.VMEM((n_z, *part), BF16),
            pltpu.VMEM(part, F32),
            pltpu.VMEM(part, F32),
            pltpu.VMEM((n_row, *part), BF16),
            pltpu.SemaphoreType.DMA((copies,)),
            pltpu.SemaphoreType.DMA((copies,)),
            pltpu.SemaphoreType.DMA((2, n_z, PIECES)),
            pltpu.SemaphoreType.DMA((2, n_z, PIECES)),
            pltpu.SemaphoreType.DMA((2, n_z, PIECES)),
            pltpu.SemaphoreType.DMA((2, n_z, PIECES)),
        ],
        compiler_params=pltpu.CompilerParams(
            collective_id=0, has_side_effects=True, vmem_limit_bytes=48 * 2**20
        ),
        name="layer",
    )(*panel, weight, cotangent, dense)
    return pl.pallas_call(
        finish_kernel,
        out_shape=shapes,
        in_specs=[vmem] * 3,
        out_specs=(pl.BlockSpec(memory_space=pltpu.HBM),) * 3,
        scratch_shapes=[pltpu.SemaphoreType.DMA((3,))],
        compiler_params=pltpu.CompilerParams(vmem_limit_bytes=2 * 2**20),
        name="finish",
    )(*results)


def solution(mesh):
    in_specs = (
        P(("row", "col"), None),
        P(),
        P(("row", "col"), None),
        P("row", "col", None),
        P("row", "col", None),
        P("row", "col"),
        P("row", "col", None, None, None),
    )
    out_specs = (P(("row", "col"), None), P(("row", "col"), None), P())
    grid = (mesh.shape["row"], mesh.shape["col"])
    body = dense_per_device if grid == (4, 8) else per_device
    return jax.shard_map(
        body, mesh=mesh, in_specs=in_specs, out_specs=out_specs, check_vma=False
    )
```

```python
import functools

import jax
import jax.numpy as jnp
from jax import lax
from jax.experimental import pallas as pl
from jax.experimental.pallas import tpu as pltpu
from jax.sharding import PartitionSpec as P


def block_sums(count, values, sources, source_of, target_of, targets, dims):
    def add(e, total):
        value = lax.dynamic_index_in_dim(values, e, keepdims=False)
        source = lax.dynamic_index_in_dim(sources, source_of[e], keepdims=False)
        prod = lax.dot_general(value, source, dims, preferred_element_type=jnp.float32)
        there = lax.dynamic_index_in_dim(total, target_of[e], keepdims=False)
        return lax.dynamic_update_index_in_dim(total, there + prod, target_of[e], 0)

    start = jnp.zeros((targets, values.shape[1], sources.shape[2]), jnp.float32)
    total = lax.fori_loop(0, count, add, start)
    return total.reshape(targets * total.shape[1], total.shape[2])


def per_device(feats, weight, cotangent, tile_rows, tile_cols, counts, block_values):
    width = feats.shape[1]
    block = block_values.shape[3]
    rows_here = tile_rows[0, 0]
    cols_here = tile_cols[0, 0]
    count = counts[0, 0]
    values = block_values[0, 0]
    row_count = lax.axis_size("row")
    col_count = lax.axis_size("col")
    own_blocks = feats.shape[0] // block
    nodes = feats.shape[0] * row_count * col_count
    panel = lax.all_gather(feats, "row", axis=0, tiled=True).reshape(
        row_count * own_blocks, block, width
    )
    partial_value = block_sums(
        count, values, panel, cols_here, rows_here, col_count * own_blocks, (((1,), (0,)), ((), ()))
    )
    agg_sum = lax.psum_scatter(partial_value, "col", scatter_dimension=0, tiled=True)
    agg = agg_sum.astype(jnp.bfloat16)
    pre = jnp.dot(agg, weight, preferred_element_type=jnp.float32)
    sig = jax.nn.sigmoid(pre)
    activated = (pre * sig).astype(jnp.bfloat16)
    dpre = (cotangent.astype(jnp.float32) * sig * (1.0 + pre * (1.0 - sig))).astype(jnp.bfloat16)
    local_term = jnp.dot(agg.T, dpre, preferred_element_type=jnp.float32)
    summed_weight = lax.psum(local_term, ("row", "col"))
    grad_weight = summed_weight * float(nodes) ** (-0.5)
    dagg = jnp.dot(dpre, weight.T, preferred_element_type=jnp.float32).astype(jnp.bfloat16)
    group = lax.all_gather(dagg, "col", axis=0, tiled=True)
    group_blocks = group.reshape(col_count * own_blocks, block, width)
    back_partial = block_sums(
        count, values, group_blocks, rows_here, cols_here, row_count * own_blocks, (((0,), (0,)), ((), ()))
    )
    grad_sum = lax.psum_scatter(back_partial, "row", scatter_dimension=0, tiled=True)
    grad_feats = grad_sum.astype(jnp.bfloat16)
    return (activated, grad_feats, grad_weight)


MESH = pl.DeviceIdType.MESH
F32 = jnp.float32
BF16 = jnp.bfloat16
CHUNKS = 20
TOGETHER = 4
PIECES = 4


def mm(a, b):
    return jnp.dot(a, b, preferred_element_type=F32)


def densify_kernel(n_cols, places_hbm, values, dense, held, acc, places, final, found, before, sems):
    most, block, _ = values.shape
    size = most // CHUNKS
    slots = dense.shape[0] * n_cols
    listed = pltpu.make_async_copy(places_hbm, places, sems.at[CHUNKS])
    listed.start()
    copies = []
    for k in range(CHUNKS):
        span = pl.ds(k * size, size)
        copies.append(pltpu.make_async_copy(values.at[span], held.at[span], sems.at[k]))
        copies[-1].start()

    def clear(i, carry):
        dense[i] = jnp.zeros(dense.shape[1:], BF16)
        return carry

    lax.fori_loop(0, dense.shape[0], clear, 0)
    for p in range(slots + 1):
        final[p] = 0
        found[p] = 0
    listed.wait()

    def mark(e, carry):
        place = places[0, e]
        before[e] = final[place]
        final[place] = e
        found[place] = found[place] + 1
        return carry

    lax.fori_loop(0, most, mark, 0, unroll=4)

    def add(e, carry):
        place = places[0, e]
        number = found[place]
        row = place // n_cols
        columns = pl.ds(pl.multiple_of(place % n_cols * block, block), block)

        def put(depth):
            at, total = e, held[e].astype(F32)
            for _ in range(depth):
                at = before[at]
                total += held[at].astype(F32)
            return before[at], total

        @pl.when((place < slots) & (final[place] == e))
        def _():
            for depth in range(TOGETHER):

                @pl.when(number == depth + 1)
                def _():
                    dense[row, :, columns] = put(depth)[1].astype(BF16)

            @pl.when(number > TOGETHER)
            def _():
                at, acc[...] = put(TOGETHER - 1)

                def more(_, at):
                    acc[...] += held[at].astype(F32)
                    return before[at]

                lax.fori_loop(TOGETHER, number, more, at)
                dense[row, :, columns] = acc[...].astype(BF16)

        return carry

    for k in range(CHUNKS):
        copies[k].wait()
        lax.fori_loop(k * size, (k + 1) * size, add, 0)


def densify(n_rows, n_cols, tile_rows, tile_cols, counts, values):
    most, block, _ = values.shape
    slots = n_rows * n_cols
    live = jnp.arange(most, dtype=jnp.int32) < counts[0, 0]
    own = lax.axis_index("row")
    places = jnp.where(live, tile_rows[0] * n_cols + (tile_cols[0] ^ own), slots)
    anywhere = pl.BlockSpec(memory_space=pltpu.HBM)
    return pl.pallas_call(
        functools.partial(densify_kernel, n_cols),
        out_shape=jax.ShapeDtypeStruct((n_rows, block, n_cols * block), BF16),
        in_specs=[anywhere] * 2,
        out_specs=pl.BlockSpec(memory_space=pltpu.VMEM),
        scratch_shapes=[
            pltpu.VMEM((most, block, block), BF16),
            pltpu.VMEM((block, block), F32),
            pltpu.SMEM(places.shape, jnp.int32),
            pltpu.SMEM((slots + 1,), jnp.int32),
            pltpu.SMEM((slots + 1,), jnp.int32),
            pltpu.SMEM((most,), jnp.int32),
            pltpu.SemaphoreType.DMA((CHUNKS + 1,)),
        ],
        compiler_params=pltpu.CompilerParams(vmem_limit_bytes=48 * 2**20),
        name="densify",
    )(places, values)


def layer_kernel(n_row, n_col, scale, *refs):
    panel, refs = refs[:n_row], refs[n_row:]
    (
        weight, cot, dense, act, gf, gw,
        xsend, xrecv, own, zsend, zrecv, group, back, bsend, brecv, ysend, yrecv, aggs, dpres, turned,
        w1send, w1recv, w2, w2send, w2recv, w3, whole, send_sems, recv_sems,
        line_send, line_recv, pair_send, pair_recv,
    ) = refs
    r = lax.axis_index("row")
    c = lax.axis_index("col")
    core = r + 1 - 2 * (r % 2)
    across = (r + 2) % n_row
    xpeer = c + 1 - 2 * (c % 2)
    x = c % 2
    z = c // 2
    n_z = n_col // 2
    inner = ((z + 1) // 2) % 2
    partners = {0: z, 1: z + 1 - 2 * (z % 2), 2: (z + 2) % n_z, 3: n_z - 1 - z}
    block, width = cot.shape
    thin = block // PIECES
    half = width // 2
    started = []

    def send(src, dst, row, col):
        k = len(started)
        copy = pltpu.make_async_remote_copy(
            src_ref=src, dst_ref=dst, send_sem=send_sems.at[k], recv_sem=recv_sems.at[k],
            device_id=(row, col), device_id_type=MESH,
        )
        copy.start()
        started.append(copy)
        return copy

    barrier = pltpu.get_barrier_semaphore()
    for k in range(1, n_row):
        pl.semaphore_signal(barrier, inc=1, device_id=((r + k) % n_row, c), device_id_type=MESH)
        pl.semaphore_signal(barrier, inc=1, device_id=((r + k) % n_row, xpeer), device_id_type=MESH)
    for k in range(1, n_col):
        pl.semaphore_signal(barrier, inc=1, device_id=(r, (c + k) % n_col), device_id_type=MESH)
    order = (3, 2, 1, 0)

    def forward(h, side):
        span = pl.ds(h * thin, thin)
        left = jnp.concatenate([dense[partners[k] * 2 + side, span] for k in order], axis=0)
        right = jnp.concatenate([p[...] for p in panel], axis=0)
        return mm(left, right)

    for h in range(PIECES):
        terms = forward(h, 1 - x).astype(BF16)
        for n, k in enumerate(order):
            xsend[h, k] = terms[n * thin : (n + 1) * thin]
    for h in range(PIECES):
        terms = forward(h, x)
        for n, k in enumerate(order):
            own[h, k] = terms[n * thin : (n + 1) * thin]
    turned[...] = weight[...].T
    pl.semaphore_wait(barrier, 2 * n_row + n_col - 3)
    halves, arrivals = {}, {}
    for h in range(PIECES):
        for k in order:
            halves[h, k] = send(xsend.at[h, k], xrecv.at[h, k], r, xpeer)

    def reduce_pair(h):
        for k in order[:-1]:
            halves[h, k].wait_recv()
            zsend[h, k] = (own[h, k] + xrecv[h, k].astype(F32)).astype(BF16)
            arrivals[h, k] = send(zsend.at[h, k], zrecv.at[h, k], r, partners[k] * 2 + x)

    def hop(g, slot, source, there, q):
        return pltpu.make_async_remote_copy(
            src_ref=group.at[g, source], dst_ref=group.at[g, source],
            send_sem=line_send.at[g, slot], recv_sem=line_recv.at[g, q],
            device_id=(r, there * 2 + x), device_id_type=MESH,
        )

    def near(g):
        return hop(g, 1, c, partners[1], 1)

    def far(g):
        there = inner * partners[3] + (1 - inner) * partners[2]
        return hop(g, 0, c, there, 2 + inner)

    def relay(g, q):
        return hop(g, q, partners[q] * 2 + x, partners[1], 5 - q)

    def straight(g, q):
        return hop(g, q, c, partners[q], q)

    def arrival(g, q):
        return hop(g, q, partners[q] * 2 + x, partners[q], q)

    def over(g, q, side):
        source = partners[q] * 2 + side
        return pltpu.make_async_remote_copy(
            src_ref=group.at[g, source], dst_ref=group.at[g, source],
            send_sem=pair_send.at[g, q], recv_sem=pair_recv.at[g, q],
            device_id=(r, xpeer), device_id_type=MESH,
        )

    def settle(g):
        halves[g, 0].wait_recv()
        total = own[g, 0] + xrecv[g, 0].astype(F32)
        for k in order[:-1]:
            arrivals[g, k].wait_recv()
            total += zrecv[g, k].astype(F32)
        span = pl.ds(g * thin, thin)
        agg = total.astype(BF16)
        pre = mm(agg, weight[...])
        sig = jax.nn.sigmoid(pre)
        dpre = (cot[span].astype(F32) * sig * (1.0 + pre * (1.0 - sig))).astype(BF16)
        group[g, c] = mm(dpre, turned[...]).astype(BF16)
        if g < PIECES - 1:
            far(g).start()
            near(g).start()
        else:
            for q in (3, 2, 1):
                straight(g, q).start()
        over(g, 0, x).start()
        act[span] = (pre * sig).astype(BF16)
        aggs[span] = agg
        dpres[span] = dpre

    def take(g, q):
        arrival(g, q).wait_recv()
        over(g, q, x).start()

    def inner_take(*places):
        @pl.when(inner == 1)
        def _():
            for q, g in places:
                arrival(g, q).wait_recv()
                if g < PIECES - 1:
                    relay(g, q).start()
                over(g, q, x).start()

    def outer_take(*places):
        @pl.when(inner == 0)
        def _():
            for q, g in places:
                take(g, q)

    turn = (((0,), (0,)), ((), ()))
    every = (0, 1, 2, 3)

    def backward(g, side, feature, places):
        span = pl.ds(g * thin, thin)
        left = jnp.concatenate([group[g, partners[q] * 2 + side, :, feature] for q in every], axis=0)
        right = jnp.concatenate([dense[partners[q] * 2 + side, span, places] for q in every], axis=0)
        return lax.dot_general(left, right, turn, preferred_element_type=F32)

    def crossed(g):
        for q in every:
            over(g, q, 1 - x).wait_recv()

    def weight_sum(stage):
        for copy in stages[stage - 1]:
            copy.wait_recv()
        if stage == 1:
            total = w1send[r].astype(F32)
            for k in range(1, n_row):
                total += w1recv[k].astype(F32)
            w2[...] = total.reshape(w2.shape)
            w2send[...] = w2[1 - x].astype(BF16)
            stages.append([send(w2send, w2recv, r, xpeer)])
        elif stage == 2:
            w3[z] = (w2[x] + w2recv[...].astype(F32)).astype(BF16)
            stages.append([send(w3.at[z], w3.at[z], r, (c + 2 * k) % n_col) for k in range(1, n_z)])
        elif stage == 3:
            total = w3[0].astype(F32)
            for k in range(1, n_z):
                total += w3[k].astype(F32)
            whole[r, x] = (total * scale).astype(BF16)
            mine = whole.at[r, x]
            stages.append([send(mine, mine, (r + k) % n_row, c) for k in range(1, n_row)])
            stages[-1].append(send(mine, mine, r, xpeer))
            stages[-1] += [send(mine, mine, (r + k) % n_row, xpeer) for k in range(1, n_row)]

    full = slice(None)
    for h in range(PIECES):
        reduce_pair(h)
    for h in range(PIECES):
        settle(h)
    term = lax.dot_general(aggs[...], dpres[...], turn, preferred_element_type=F32)
    part = term.shape[0] // n_row
    for k in range(n_row):
        w1send[k] = term[k * part : (k + 1) * part].astype(BF16)
    stages = [
        [send(w1send.at[(r + k) % n_row], w1recv.at[k], (r + k) % n_row, c) for k in range(1, n_row)]
    ]
    for g in range(PIECES - 1):
        take(g, 1)
        inner_take((3, g), (2, g))
    outer_take((2, 0), (3, 0))
    weight_sum(1)
    take(3, 1)
    inner_take((3, 3), (2, 3))
    outer_take((2, 1), (3, 1), (3, 3), (2, 3), (2, 2), (3, 2))
    weight_sum(2)
    for g in range(PIECES):
        back[...] = (back[...] if g else 0.0) + backward(g, x, full, full)
    for g in range(PIECES - 1):
        crossed(g)
        back[...] += backward(g, 1 - x, full, full)
    crossed(3)

    def place(p):
        return pl.ds(p * block, block)

    seconds, lasts = [], []
    spans = [pl.ds(f * half, half) for f in range(2)]
    for rows_f in spans:
        bsend[1, rows_f] = back[rows_f, place(3)] + backward(3, 1 - x, rows_f, place(3))
        seconds.append(send(bsend.at[1, rows_f], brecv.at[1, rows_f], core, c))
    ahead = back[:, place(2)] + backward(3, 1 - x, full, place(2))
    for f, rows_f in enumerate(spans):
        seconds[f].wait_recv()
        ysend[rows_f] = (ahead[f * half : (f + 1) * half] + brecv[1, rows_f]).astype(BF16)
        lasts.append(send(ysend.at[rows_f], yrecv.at[rows_f], across, c))
    weight_sum(3)
    bsend[0] = back[:, place(1)] + backward(3, 1 - x, full, place(1))
    first = send(bsend.at[0], brecv.at[0], core, c)
    total = back[:, place(0)] + backward(3, 1 - x, full, place(0))
    first.wait_recv()
    total += brecv[0]
    for copy in lasts:
        copy.wait_recv()
    total += yrecv[...].astype(F32)
    gf[...] = total.T.astype(BF16)
    weight_sum(4)
    gw[...] = whole[...].astype(F32).reshape(gw.shape)
    for copy in started:
        copy.wait_send()
    for g in range(PIECES):
        for q in range(n_z):
            over(g, q, x).wait_send()
        if g < PIECES - 1:
            near(g).wait_send()
            far(g).wait_send()

            @pl.when(inner == 1)
            def _():
                for q in (2, 3):
                    relay(g, q).wait_send()
        else:
            for q in (3, 2, 1):
                straight(g, q).wait_send()


def finish_kernel(act, gf, gw, act_out, gf_out, gw_out, sems):
    copies = []
    for k, (src, dst) in enumerate(((act, act_out), (gf, gf_out), (gw, gw_out))):
        copies.append(pltpu.make_async_copy(src, dst, sems.at[k]))
        copies[-1].start()
    for copy in copies:
        copy.wait()


def dense_per_device(feats, weight, cotangent, tile_rows, tile_cols, counts, block_values):
    n_row = lax.axis_size("row")
    n_col = lax.axis_size("col")
    block, width = feats.shape
    dense = densify(n_col, n_row, tile_rows, tile_cols, counts, block_values[0, 0])
    scale = float(block * n_row * n_col) ** -0.5
    panel = [feats] + [
        lax.ppermute(feats, "row", [(i, i ^ k) for i in range(n_row)])
        for k in range(1, n_row)
    ]
    n_z = n_col // 2
    tile = (block, width)
    part = (width // n_row, width)
    slim = (part[0] // 2, width)
    thin = (block // PIECES, width)
    copies = PIECES * (2 * n_z - 1) + 3 * n_row - 2 + n_z + 5
    vmem = pl.BlockSpec(memory_space=pltpu.VMEM)
    shapes = (
        jax.ShapeDtypeStruct(tile, BF16),
        jax.ShapeDtypeStruct(tile, BF16),
        jax.ShapeDtypeStruct((width, width), F32),
    )
    results = pl.pallas_call(
        functools.partial(layer_kernel, n_row, n_col, scale),
        out_shape=shapes,
        in_specs=[vmem] * (n_row + 3),
        out_specs=(vmem, vmem, vmem),
        scratch_shapes=[
            pltpu.VMEM((PIECES, n_z, *thin), BF16),
            pltpu.VMEM((PIECES, n_z, *thin), BF16),
            pltpu.VMEM((PIECES, n_z, *thin), F32),
            pltpu.VMEM((PIECES, n_z, *thin), BF16),
            pltpu.VMEM((PIECES, n_z, *thin), BF16),
            pltpu.VMEM((PIECES, n_col, *thin), BF16),
            pltpu.VMEM((width, n_row * block), F32),
            pltpu.VMEM((2, *tile), F32),
            pltpu.VMEM((2, *tile), F32),
            pltpu.VMEM(tile, BF16),
            pltpu.VMEM(tile, BF16),
            pltpu.VMEM(tile, BF16),
            pltpu.VMEM(tile, BF16),
            pltpu.VMEM((width, width), BF16),
            pltpu.VMEM((n_row, *part), BF16),
            pltpu.VMEM((n_row, *part), BF16),
            pltpu.VMEM((2, *slim), F32),
            pltpu.VMEM(slim, BF16),
            pltpu.VMEM(slim, BF16),
            pltpu.VMEM((n_z, *slim), BF16),
            pltpu.VMEM((n_row, 2, *slim), BF16),
            pltpu.SemaphoreType.DMA((copies,)),
            pltpu.SemaphoreType.DMA((copies,)),
            pltpu.SemaphoreType.DMA((PIECES, n_z)),
            pltpu.SemaphoreType.DMA((PIECES, n_z)),
            pltpu.SemaphoreType.DMA((PIECES, n_z)),
            pltpu.SemaphoreType.DMA((PIECES, n_z)),
        ],
        compiler_params=pltpu.CompilerParams(
            collective_id=0, has_side_effects=True, vmem_limit_bytes=48 * 2**20
        ),
        name="layer",
    )(*panel, weight, cotangent, dense)
    return pl.pallas_call(
        finish_kernel,
        out_shape=shapes,
        in_specs=[vmem] * 3,
        out_specs=(pl.BlockSpec(memory_space=pltpu.HBM),) * 3,
        scratch_shapes=[pltpu.SemaphoreType.DMA((3,))],
        compiler_params=pltpu.CompilerParams(vmem_limit_bytes=2 * 2**20),
        name="finish",
    )(*results)


def solution(mesh):
    in_specs = (
        P(("row", "col"), None),
        P(),
        P(("row", "col"), None),
        P("row", "col", None),
        P("row", "col", None),
        P("row", "col"),
        P("row", "col", None, None, None),
    )
    out_specs = (P(("row", "col"), None), P(("row", "col"), None), P())
    grid = (mesh.shape["row"], mesh.shape["col"])
    body = dense_per_device if grid == (4, 8) else per_device
    return jax.shard_map(
        body, mesh=mesh, in_specs=in_specs, out_specs=out_specs, check_vma=False
    )
```

```python
import functools

import jax
import jax.numpy as jnp
from jax import lax
from jax.experimental import pallas as pl
from jax.experimental.pallas import tpu as pltpu
from jax.sharding import PartitionSpec as P


def block_sums(count, values, sources, source_of, target_of, targets, dims):
    def add(e, total):
        value = lax.dynamic_index_in_dim(values, e, keepdims=False)
        source = lax.dynamic_index_in_dim(sources, source_of[e], keepdims=False)
        prod = lax.dot_general(value, source, dims, preferred_element_type=jnp.float32)
        there = lax.dynamic_index_in_dim(total, target_of[e], keepdims=False)
        return lax.dynamic_update_index_in_dim(total, there + prod, target_of[e], 0)

    start = jnp.zeros((targets, values.shape[1], sources.shape[2]), jnp.float32)
    total = lax.fori_loop(0, count, add, start)
    return total.reshape(targets * total.shape[1], total.shape[2])


def per_device(feats, weight, cotangent, tile_rows, tile_cols, counts, block_values):
    width = feats.shape[1]
    block = block_values.shape[3]
    rows_here = tile_rows[0, 0]
    cols_here = tile_cols[0, 0]
    count = counts[0, 0]
    values = block_values[0, 0]
    row_count = lax.axis_size("row")
    col_count = lax.axis_size("col")
    own_blocks = feats.shape[0] // block
    nodes = feats.shape[0] * row_count * col_count
    panel = lax.all_gather(feats, "row", axis=0, tiled=True).reshape(
        row_count * own_blocks, block, width
    )
    partial_value = block_sums(
        count, values, panel, cols_here, rows_here, col_count * own_blocks, (((1,), (0,)), ((), ()))
    )
    agg_sum = lax.psum_scatter(partial_value, "col", scatter_dimension=0, tiled=True)
    agg = agg_sum.astype(jnp.bfloat16)
    pre = jnp.dot(agg, weight, preferred_element_type=jnp.float32)
    sig = jax.nn.sigmoid(pre)
    activated = (pre * sig).astype(jnp.bfloat16)
    dpre = (cotangent.astype(jnp.float32) * sig * (1.0 + pre * (1.0 - sig))).astype(jnp.bfloat16)
    local_term = jnp.dot(agg.T, dpre, preferred_element_type=jnp.float32)
    summed_weight = lax.psum(local_term, ("row", "col"))
    grad_weight = summed_weight * float(nodes) ** (-0.5)
    dagg = jnp.dot(dpre, weight.T, preferred_element_type=jnp.float32).astype(jnp.bfloat16)
    group = lax.all_gather(dagg, "col", axis=0, tiled=True)
    group_blocks = group.reshape(col_count * own_blocks, block, width)
    back_partial = block_sums(
        count, values, group_blocks, rows_here, cols_here, row_count * own_blocks, (((0,), (0,)), ((), ()))
    )
    grad_sum = lax.psum_scatter(back_partial, "row", scatter_dimension=0, tiled=True)
    grad_feats = grad_sum.astype(jnp.bfloat16)
    return (activated, grad_feats, grad_weight)


MESH = pl.DeviceIdType.MESH
F32 = jnp.float32
BF16 = jnp.bfloat16
CHUNKS = 10
PIECES = 4


def mm(a, b):
    return jnp.dot(a, b, preferred_element_type=F32)


def densify_kernel(places_hbm, values, acc, held, places, sems):
    most = values.shape[0]
    size = most // CHUNKS
    listed = pltpu.make_async_copy(places_hbm, places, sems.at[CHUNKS])
    listed.start()
    copies = []
    for k in range(CHUNKS):
        span = pl.ds(k * size, size)
        copies.append(pltpu.make_async_copy(values.at[span], held.at[span], sems.at[k]))
        copies[-1].start()

    def clear(p, carry):
        acc[p] = jnp.zeros(acc.shape[1:], F32)
        return carry

    lax.fori_loop(0, acc.shape[0], clear, 0)
    listed.wait()

    def add(e, carry):
        acc[places[0, e]] += held[e].astype(F32)
        return carry

    for k in range(CHUNKS):
        copies[k].wait()
        lax.fori_loop(k * size, (k + 1) * size, add, 0)


def densify(n_rows, n_cols, tile_rows, tile_cols, counts, values):
    most, block, _ = values.shape
    slots = n_rows * n_cols
    live = jnp.arange(most, dtype=jnp.int32) < counts[0, 0]
    own = lax.axis_index("row")
    places = jnp.where(live, tile_rows[0] * n_cols + (tile_cols[0] ^ own), slots)
    anywhere = pl.BlockSpec(memory_space=pltpu.HBM)
    return pl.pallas_call(
        densify_kernel,
        out_shape=jax.ShapeDtypeStruct((slots + 1, block, block), F32),
        in_specs=[anywhere] * 2,
        out_specs=pl.BlockSpec(memory_space=pltpu.VMEM),
        scratch_shapes=[
            pltpu.VMEM((most, block, block), BF16),
            pltpu.SMEM(places.shape, jnp.int32),
            pltpu.SemaphoreType.DMA((CHUNKS + 1,)),
        ],
        compiler_params=pltpu.CompilerParams(vmem_limit_bytes=36 * 2**20),
        name="densify",
    )(places, values)


def layer_kernel(n_row, n_col, scale, *refs):
    panel, refs = refs[:n_row], refs[n_row:]
    (
        weight, cot, summed, act, gf, gw,
        dense, xsend, xrecv, own, zsend, zrecv, group, back, bsend, brecv, ysend, yrecv, aggs, dpres, turned,
        w1send, w1recv, w2, w2send, w2recv, w3, whole, send_sems, recv_sems,
        line_send, line_recv, pair_send, pair_recv,
    ) = refs
    r = lax.axis_index("row")
    c = lax.axis_index("col")
    core = r + 1 - 2 * (r % 2)
    across = (r + 2) % n_row
    xpeer = c + 1 - 2 * (c % 2)
    x = c % 2
    z = c // 2
    n_z = n_col // 2
    inner = ((z + 1) // 2) % 2
    partners = {0: z, 1: z + 1 - 2 * (z % 2), 2: (z + 2) % n_z, 3: n_z - 1 - z}
    block, width = cot.shape
    thin = block // PIECES
    half = width // 2
    started = []

    def send(src, dst, row, col):
        k = len(started)
        copy = pltpu.make_async_remote_copy(
            src_ref=src, dst_ref=dst, send_sem=send_sems.at[k], recv_sem=recv_sems.at[k],
            device_id=(row, col), device_id_type=MESH,
        )
        copy.start()
        started.append(copy)
        return copy

    barrier = pltpu.get_barrier_semaphore()
    for k in range(1, n_row):
        pl.semaphore_signal(barrier, inc=1, device_id=((r + k) % n_row, c), device_id_type=MESH)
        pl.semaphore_signal(barrier, inc=1, device_id=((r + k) % n_row, xpeer), device_id_type=MESH)
    for k in range(1, n_col):
        pl.semaphore_signal(barrier, inc=1, device_id=(r, (c + k) % n_col), device_id_type=MESH)
    def settle_block(i, carry):
        for p in range(n_row):
            dense[i, :, p * block : (p + 1) * block] = summed[i * n_row + p].astype(BF16)
        return carry

    lax.fori_loop(0, n_col, settle_block, 0)
    order = (3, 2, 1, 0)

    def forward(h, side):
        span = pl.ds(h * thin, thin)
        left = jnp.concatenate([dense[partners[k] * 2 + side, span] for k in order], axis=0)
        right = jnp.concatenate([p[...] for p in panel], axis=0)
        return mm(left, right)

    for h in range(PIECES):
        terms = forward(h, 1 - x).astype(BF16)
        for n, k in enumerate(order):
            xsend[h, k] = terms[n * thin : (n + 1) * thin]
    for h in range(PIECES):
        terms = forward(h, x)
        for n, k in enumerate(order):
            own[h, k] = terms[n * thin : (n + 1) * thin]
    turned[...] = weight[...].T
    pl.semaphore_wait(barrier, 2 * n_row + n_col - 3)
    halves, arrivals = {}, {}
    for h in range(PIECES):
        for k in order:
            halves[h, k] = send(xsend.at[h, k], xrecv.at[h, k], r, xpeer)

    def reduce_pair(h):
        for k in order[:-1]:
            halves[h, k].wait_recv()
            zsend[h, k] = (own[h, k] + xrecv[h, k].astype(F32)).astype(BF16)
            arrivals[h, k] = send(zsend.at[h, k], zrecv.at[h, k], r, partners[k] * 2 + x)

    def hop(g, slot, source, there, q):
        return pltpu.make_async_remote_copy(
            src_ref=group.at[g, source], dst_ref=group.at[g, source],
            send_sem=line_send.at[g, slot], recv_sem=line_recv.at[g, q],
            device_id=(r, there * 2 + x), device_id_type=MESH,
        )

    def near(g):
        return hop(g, 1, c, partners[1], 1)

    def far(g):
        there = inner * partners[3] + (1 - inner) * partners[2]
        return hop(g, 0, c, there, 2 + inner)

    def relay(g, q):
        return hop(g, q, partners[q] * 2 + x, partners[1], 5 - q)

    def straight(g, q):
        return hop(g, q, c, partners[q], q)

    def arrival(g, q):
        return hop(g, q, partners[q] * 2 + x, partners[q], q)

    def over(g, q, side):
        source = partners[q] * 2 + side
        return pltpu.make_async_remote_copy(
            src_ref=group.at[g, source], dst_ref=group.at[g, source],
            send_sem=pair_send.at[g, q], recv_sem=pair_recv.at[g, q],
            device_id=(r, xpeer), device_id_type=MESH,
        )

    def settle(g):
        halves[g, 0].wait_recv()
        total = own[g, 0] + xrecv[g, 0].astype(F32)
        for k in order[:-1]:
            arrivals[g, k].wait_recv()
            total += zrecv[g, k].astype(F32)
        span = pl.ds(g * thin, thin)
        agg = total.astype(BF16)
        pre = mm(agg, weight[...])
        sig = jax.nn.sigmoid(pre)
        dpre = (cot[span].astype(F32) * sig * (1.0 + pre * (1.0 - sig))).astype(BF16)
        group[g, c] = mm(dpre, turned[...]).astype(BF16)
        if g == 0:
            far(g).start()
        if g < PIECES - 1:
            near(g).start()
        else:
            for early in range(1, g):
                far(early).start()
            for q in (3, 2, 1):
                straight(g, q).start()
        over(g, 0, x).start()
        act[span] = (pre * sig).astype(BF16)
        aggs[span] = agg
        dpres[span] = dpre

    def take(g, q):
        arrival(g, q).wait_recv()
        over(g, q, x).start()

    def inner_take(*places):
        @pl.when(inner == 1)
        def _():
            for q, g in places:
                arrival(g, q).wait_recv()
                if g < PIECES - 1:
                    relay(g, q).start()
                over(g, q, x).start()

    def outer_take(*places):
        @pl.when(inner == 0)
        def _():
            for q, g in places:
                take(g, q)

    turn = (((0,), (0,)), ((), ()))
    every = (0, 1, 2, 3)

    def backward(g, side, feature, places):
        span = pl.ds(g * thin, thin)
        left = jnp.concatenate([group[g, partners[q] * 2 + side, :, feature] for q in every], axis=0)
        right = jnp.concatenate([dense[partners[q] * 2 + side, span, places] for q in every], axis=0)
        return lax.dot_general(left, right, turn, preferred_element_type=F32)

    def crossed(g):
        for q in every:
            over(g, q, 1 - x).wait_recv()

    def weight_sum(stage):
        for copy in stages[stage - 1]:
            copy.wait_recv()
        if stage == 1:
            total = w1send[r].astype(F32)
            for k in range(1, n_row):
                total += w1recv[k].astype(F32)
            w2[...] = total.reshape(w2.shape)
            w2send[...] = w2[1 - x].astype(BF16)
            stages.append([send(w2send, w2recv, r, xpeer)])
        elif stage == 2:
            w3[z] = (w2[x] + w2recv[...].astype(F32)).astype(BF16)
            stages.append([send(w3.at[z], w3.at[z], r, (c + 2 * k) % n_col) for k in range(1, n_z)])
        elif stage == 3:
            total = w3[0].astype(F32)
            for k in range(1, n_z):
                total += w3[k].astype(F32)
            whole[r, x] = (total * scale).astype(BF16)
            mine = whole.at[r, x]
            stages.append([send(mine, mine, (r + k) % n_row, c) for k in range(1, n_row)])
            stages[-1].append(send(mine, mine, r, xpeer))
            stages[-1] += [send(mine, mine, (r + k) % n_row, xpeer) for k in range(1, n_row)]

    full = slice(None)
    for h in range(PIECES):
        reduce_pair(h)
    for h in range(PIECES):
        settle(h)
    term = lax.dot_general(aggs[...], dpres[...], turn, preferred_element_type=F32)
    part = term.shape[0] // n_row
    for k in range(n_row):
        w1send[k] = term[k * part : (k + 1) * part].astype(BF16)
    stages = [
        [send(w1send.at[(r + k) % n_row], w1recv.at[k], (r + k) % n_row, c) for k in range(1, n_row)]
    ]
    for g in range(PIECES - 1):
        take(g, 1)
        inner_take((3, g), (2, g))
    outer_take((2, 0), (3, 0))
    take(3, 1)
    inner_take((3, 3), (2, 3))
    weight_sum(1)
    outer_take((2, 1), (3, 1), (3, 3), (2, 3), (2, 2), (3, 2))
    weight_sum(2)
    for g in range(PIECES):
        back[...] = (back[...] if g else 0.0) + backward(g, x, full, full)
    for g in range(PIECES - 1):
        crossed(g)
        back[...] += backward(g, 1 - x, full, full)
    crossed(3)

    def place(p):
        return pl.ds(p * block, block)

    seconds, lasts = [], []
    spans = [pl.ds(f * half, half) for f in range(2)]
    for rows_f in spans:
        bsend[1, rows_f] = back[rows_f, place(3)] + backward(3, 1 - x, rows_f, place(3))
        seconds.append(send(bsend.at[1, rows_f], brecv.at[1, rows_f], core, c))
    ahead = back[:, place(2)] + backward(3, 1 - x, full, place(2))
    for f, rows_f in enumerate(spans):
        seconds[f].wait_recv()
        ysend[rows_f] = (ahead[f * half : (f + 1) * half] + brecv[1, rows_f]).astype(BF16)
        lasts.append(send(ysend.at[rows_f], yrecv.at[rows_f], across, c))
    bsend[0] = back[:, place(1)] + backward(3, 1 - x, full, place(1))
    first = send(bsend.at[0], brecv.at[0], core, c)
    total = back[:, place(0)] + backward(3, 1 - x, full, place(0))
    first.wait_recv()
    total += brecv[0]
    weight_sum(3)
    for copy in lasts:
        copy.wait_recv()
    total += yrecv[...].astype(F32)
    gf[...] = total.T.astype(BF16)
    weight_sum(4)
    gw[...] = whole[...].astype(F32).reshape(gw.shape)
    for copy in started:
        copy.wait_send()
    for g in range(PIECES):
        for q in range(n_z):
            over(g, q, x).wait_send()
        if g < PIECES - 1:
            near(g).wait_send()
            far(g).wait_send()

            @pl.when(inner == 1)
            def _():
                for q in (2, 3):
                    relay(g, q).wait_send()
        else:
            for q in (3, 2, 1):
                straight(g, q).wait_send()


def finish_kernel(act, gf, gw, act_out, gf_out, gw_out, sems):
    copies = []
    for k, (src, dst) in enumerate(((act, act_out), (gf, gf_out), (gw, gw_out))):
        copies.append(pltpu.make_async_copy(src, dst, sems.at[k]))
        copies[-1].start()
    for copy in copies:
        copy.wait()


def dense_per_device(feats, weight, cotangent, tile_rows, tile_cols, counts, block_values):
    n_row = lax.axis_size("row")
    n_col = lax.axis_size("col")
    block, width = feats.shape
    dense = densify(n_col, n_row, tile_rows, tile_cols, counts, block_values[0, 0])
    scale = float(block * n_row * n_col) ** -0.5
    panel = [feats] + [
        lax.ppermute(feats, "row", [(i, i ^ k) for i in range(n_row)])
        for k in range(1, n_row)
    ]
    n_z = n_col // 2
    tile = (block, width)
    part = (width // n_row, width)
    slim = (part[0] // 2, width)
    thin = (block // PIECES, width)
    copies = PIECES * (2 * n_z - 1) + 3 * n_row - 2 + n_z + 5
    vmem = pl.BlockSpec(memory_space=pltpu.VMEM)
    shapes = (
        jax.ShapeDtypeStruct(tile, BF16),
        jax.ShapeDtypeStruct(tile, BF16),
        jax.ShapeDtypeStruct((width, width), F32),
    )
    results = pl.pallas_call(
        functools.partial(layer_kernel, n_row, n_col, scale),
        out_shape=shapes,
        in_specs=[vmem] * (n_row + 3),
        out_specs=(vmem, vmem, vmem),
        scratch_shapes=[
            pltpu.VMEM((n_col, block, n_row * block), BF16),
            pltpu.VMEM((PIECES, n_z, *thin), BF16),
            pltpu.VMEM((PIECES, n_z, *thin), BF16),
            pltpu.VMEM((PIECES, n_z, *thin), F32),
            pltpu.VMEM((PIECES, n_z, *thin), BF16),
            pltpu.VMEM((PIECES, n_z, *thin), BF16),
            pltpu.VMEM((PIECES, n_col, *thin), BF16),
            pltpu.VMEM((width, n_row * block), F32),
            pltpu.VMEM((2, *tile), F32),
            pltpu.VMEM((2, *tile), F32),
            pltpu.VMEM(tile, BF16),
            pltpu.VMEM(tile, BF16),
            pltpu.VMEM(tile, BF16),
            pltpu.VMEM(tile, BF16),
            pltpu.VMEM((width, width), BF16),
            pltpu.VMEM((n_row, *part), BF16),
            pltpu.VMEM((n_row, *part), BF16),
            pltpu.VMEM((2, *slim), F32),
            pltpu.VMEM(slim, BF16),
            pltpu.VMEM(slim, BF16),
            pltpu.VMEM((n_z, *slim), BF16),
            pltpu.VMEM((n_row, 2, *slim), BF16),
            pltpu.SemaphoreType.DMA((copies,)),
            pltpu.SemaphoreType.DMA((copies,)),
            pltpu.SemaphoreType.DMA((PIECES, n_z)),
            pltpu.SemaphoreType.DMA((PIECES, n_z)),
            pltpu.SemaphoreType.DMA((PIECES, n_z)),
            pltpu.SemaphoreType.DMA((PIECES, n_z)),
        ],
        compiler_params=pltpu.CompilerParams(
            collective_id=0, has_side_effects=True, vmem_limit_bytes=28 * 2**20
        ),
        name="layer",
    )(*panel, weight, cotangent, dense)
    return pl.pallas_call(
        finish_kernel,
        out_shape=shapes,
        in_specs=[vmem] * 3,
        out_specs=(pl.BlockSpec(memory_space=pltpu.HBM),) * 3,
        scratch_shapes=[pltpu.SemaphoreType.DMA((3,))],
        compiler_params=pltpu.CompilerParams(vmem_limit_bytes=2 * 2**20),
        name="finish",
    )(*results)


def solution(mesh):
    in_specs = (
        P(("row", "col"), None),
        P(),
        P(("row", "col"), None),
        P("row", "col", None),
        P("row", "col", None),
        P("row", "col"),
        P("row", "col", None, None, None),
    )
    out_specs = (P(("row", "col"), None), P(("row", "col"), None), P())
    grid = (mesh.shape["row"], mesh.shape["col"])
    body = dense_per_device if grid == (4, 8) else per_device
    return jax.shard_map(
        body, mesh=mesh, in_specs=in_specs, out_specs=out_specs, check_vma=False
    )
```

```python
import functools

import jax
import jax.numpy as jnp
from jax import lax
from jax.experimental import pallas as pl
from jax.experimental.pallas import tpu as pltpu
from jax.sharding import PartitionSpec as P


def block_sums(count, values, sources, source_of, target_of, targets, dims):
    def add(e, total):
        value = lax.dynamic_index_in_dim(values, e, keepdims=False)
        source = lax.dynamic_index_in_dim(sources, source_of[e], keepdims=False)
        prod = lax.dot_general(value, source, dims, preferred_element_type=jnp.float32)
        there = lax.dynamic_index_in_dim(total, target_of[e], keepdims=False)
        return lax.dynamic_update_index_in_dim(total, there + prod, target_of[e], 0)

    start = jnp.zeros((targets, values.shape[1], sources.shape[2]), jnp.float32)
    total = lax.fori_loop(0, count, add, start)
    return total.reshape(targets * total.shape[1], total.shape[2])


def per_device(feats, weight, cotangent, tile_rows, tile_cols, counts, block_values):
    width = feats.shape[1]
    block = block_values.shape[3]
    rows_here = tile_rows[0, 0]
    cols_here = tile_cols[0, 0]
    count = counts[0, 0]
    values = block_values[0, 0]
    row_count = lax.axis_size("row")
    col_count = lax.axis_size("col")
    own_blocks = feats.shape[0] // block
    nodes = feats.shape[0] * row_count * col_count
    panel = lax.all_gather(feats, "row", axis=0, tiled=True).reshape(
        row_count * own_blocks, block, width
    )
    partial_value = block_sums(
        count, values, panel, cols_here, rows_here, col_count * own_blocks, (((1,), (0,)), ((), ()))
    )
    agg_sum = lax.psum_scatter(partial_value, "col", scatter_dimension=0, tiled=True)
    agg = agg_sum.astype(jnp.bfloat16)
    pre = jnp.dot(agg, weight, preferred_element_type=jnp.float32)
    sig = jax.nn.sigmoid(pre)
    activated = (pre * sig).astype(jnp.bfloat16)
    dpre = (cotangent.astype(jnp.float32) * sig * (1.0 + pre * (1.0 - sig))).astype(jnp.bfloat16)
    local_term = jnp.dot(agg.T, dpre, preferred_element_type=jnp.float32)
    summed_weight = lax.psum(local_term, ("row", "col"))
    grad_weight = summed_weight * float(nodes) ** (-0.5)
    dagg = jnp.dot(dpre, weight.T, preferred_element_type=jnp.float32).astype(jnp.bfloat16)
    group = lax.all_gather(dagg, "col", axis=0, tiled=True)
    group_blocks = group.reshape(col_count * own_blocks, block, width)
    back_partial = block_sums(
        count, values, group_blocks, rows_here, cols_here, row_count * own_blocks, (((0,), (0,)), ((), ()))
    )
    grad_sum = lax.psum_scatter(back_partial, "row", scatter_dimension=0, tiled=True)
    grad_feats = grad_sum.astype(jnp.bfloat16)
    return (activated, grad_feats, grad_weight)


MESH = pl.DeviceIdType.MESH
F32 = jnp.float32
BF16 = jnp.bfloat16
CHUNKS = 10
PIECES = 4


def mm(a, b):
    return jnp.dot(a, b, preferred_element_type=F32)


def densify_kernel(places_hbm, values, acc, held, places, sems):
    most = values.shape[0]
    size = most // CHUNKS
    listed = pltpu.make_async_copy(places_hbm, places, sems.at[CHUNKS])
    listed.start()
    copies = []
    for k in range(CHUNKS):
        span = pl.ds(k * size, size)
        copies.append(pltpu.make_async_copy(values.at[span], held.at[span], sems.at[k]))
        copies[-1].start()

    def clear(p, carry):
        acc[p] = jnp.zeros(acc.shape[1:], F32)
        return carry

    lax.fori_loop(0, acc.shape[0], clear, 0)
    listed.wait()

    def add(e, carry):
        acc[places[0, e]] += held[e].astype(F32)
        return carry

    for k in range(CHUNKS):
        copies[k].wait()
        lax.fori_loop(k * size, (k + 1) * size, add, 0)


def densify(n_rows, n_cols, tile_rows, tile_cols, counts, values):
    most, block, _ = values.shape
    slots = n_rows * n_cols
    live = jnp.arange(most, dtype=jnp.int32) < counts[0, 0]
    own = lax.axis_index("row")
    places = jnp.where(live, tile_rows[0] * n_cols + (tile_cols[0] ^ own), slots)
    anywhere = pl.BlockSpec(memory_space=pltpu.HBM)
    return pl.pallas_call(
        densify_kernel,
        out_shape=jax.ShapeDtypeStruct((slots + 1, block, block), F32),
        in_specs=[anywhere] * 2,
        out_specs=pl.BlockSpec(memory_space=pltpu.VMEM),
        scratch_shapes=[
            pltpu.VMEM((most, block, block), BF16),
            pltpu.SMEM(places.shape, jnp.int32),
            pltpu.SemaphoreType.DMA((CHUNKS + 1,)),
        ],
        compiler_params=pltpu.CompilerParams(vmem_limit_bytes=36 * 2**20),
        name="densify",
    )(places, values)


def layer_kernel(n_row, n_col, scale, *refs):
    panel, refs = refs[:n_row], refs[n_row:]
    (
        weight, cot, summed, act, gf, gw,
        dense, xsend, xrecv, own, zsend, zrecv, group, back, bsend, brecv, ysend, yrecv, aggs, dpres, turned,
        w1send, w1recv, w2, w2send, w2recv, w3, whole, send_sems, recv_sems,
        line_send, line_recv, pair_send, pair_recv,
    ) = refs
    r = lax.axis_index("row")
    c = lax.axis_index("col")
    core = r + 1 - 2 * (r % 2)
    across = (r + 2) % n_row
    xpeer = c + 1 - 2 * (c % 2)
    x = c % 2
    z = c // 2
    n_z = n_col // 2
    inner = ((z + 1) // 2) % 2
    partners = {0: z, 1: z + 1 - 2 * (z % 2), 2: (z + 2) % n_z, 3: n_z - 1 - z}
    block, width = cot.shape
    thin = block // PIECES
    half = width // 2
    started = []

    def send(src, dst, row, col):
        k = len(started)
        copy = pltpu.make_async_remote_copy(
            src_ref=src, dst_ref=dst, send_sem=send_sems.at[k], recv_sem=recv_sems.at[k],
            device_id=(row, col), device_id_type=MESH,
        )
        copy.start()
        started.append(copy)
        return copy

    barrier = pltpu.get_barrier_semaphore()
    for k in range(1, n_row):
        pl.semaphore_signal(barrier, inc=1, device_id=((r + k) % n_row, c), device_id_type=MESH)
        pl.semaphore_signal(barrier, inc=1, device_id=((r + k) % n_row, xpeer), device_id_type=MESH)
    for k in range(1, n_col):
        pl.semaphore_signal(barrier, inc=1, device_id=(r, (c + k) % n_col), device_id_type=MESH)
    def settle_block(i, carry):
        for p in range(n_row):
            dense[i, :, p * block : (p + 1) * block] = summed[i * n_row + p].astype(BF16)
        return carry

    lax.fori_loop(0, n_col, settle_block, 0)
    order = (3, 2, 1, 0)

    def forward(h, side):
        span = pl.ds(h * thin, thin)
        left = jnp.concatenate([dense[partners[k] * 2 + side, span] for k in order], axis=0)
        right = jnp.concatenate([p[...] for p in panel], axis=0)
        return mm(left, right)

    for h in range(PIECES):
        terms = forward(h, 1 - x).astype(BF16)
        for n, k in enumerate(order):
            xsend[h, k] = terms[n * thin : (n + 1) * thin]
    turned[...] = weight[...].T
    pl.semaphore_wait(barrier, 2 * n_row + n_col - 3)
    halves, arrivals = {}, {}
    for h in range(PIECES):
        for k in order:
            halves[h, k] = send(xsend.at[h, k], xrecv.at[h, k], r, xpeer)
    for h in range(PIECES):
        terms = forward(h, x)
        for n, k in enumerate(order):
            own[h, k] = terms[n * thin : (n + 1) * thin]

    def reduce_pair(h):
        for k in order[:-1]:
            halves[h, k].wait_recv()
            zsend[h, k] = (own[h, k] + xrecv[h, k].astype(F32)).astype(BF16)
            arrivals[h, k] = send(zsend.at[h, k], zrecv.at[h, k], r, partners[k] * 2 + x)

    def hop(g, slot, source, there, q):
        return pltpu.make_async_remote_copy(
            src_ref=group.at[g, source], dst_ref=group.at[g, source],
            send_sem=line_send.at[g, slot], recv_sem=line_recv.at[g, q],
            device_id=(r, there * 2 + x), device_id_type=MESH,
        )

    def near(g):
        return hop(g, 1, c, partners[1], 1)

    def far(g):
        there = inner * partners[3] + (1 - inner) * partners[2]
        return hop(g, 0, c, there, 2 + inner)

    def relay(g, q):
        return hop(g, q, partners[q] * 2 + x, partners[1], 5 - q)

    def straight(g, q):
        return hop(g, q, c, partners[q], q)

    def arrival(g, q):
        return hop(g, q, partners[q] * 2 + x, partners[q], q)

    def over(g, q, side):
        source = partners[q] * 2 + side
        return pltpu.make_async_remote_copy(
            src_ref=group.at[g, source], dst_ref=group.at[g, source],
            send_sem=pair_send.at[g, q], recv_sem=pair_recv.at[g, q],
            device_id=(r, xpeer), device_id_type=MESH,
        )

    def settle(g):
        halves[g, 0].wait_recv()
        total = own[g, 0] + xrecv[g, 0].astype(F32)
        for k in order[:-1]:
            arrivals[g, k].wait_recv()
            total += zrecv[g, k].astype(F32)
        span = pl.ds(g * thin, thin)
        agg = total.astype(BF16)
        pre = mm(agg, weight[...])
        sig = jax.nn.sigmoid(pre)
        dpre = (cot[span].astype(F32) * sig * (1.0 + pre * (1.0 - sig))).astype(BF16)
        group[g, c] = mm(dpre, turned[...]).astype(BF16)
        if g == 0:
            far(g).start()
        if g < PIECES - 1:
            near(g).start()
        else:
            for early in range(1, g):
                far(early).start()
            for q in (3, 2, 1):
                straight(g, q).start()
        over(g, 0, x).start()
        act[span] = (pre * sig).astype(BF16)
        aggs[span] = agg
        dpres[span] = dpre

    def take(g, q):
        arrival(g, q).wait_recv()
        over(g, q, x).start()

    def inner_take(*places):
        @pl.when(inner == 1)
        def _():
            for q, g in places:
                arrival(g, q).wait_recv()
                if g < PIECES - 1:
                    relay(g, q).start()
                over(g, q, x).start()

    def outer_take(*places):
        @pl.when(inner == 0)
        def _():
            for q, g in places:
                take(g, q)

    turn = (((0,), (0,)), ((), ()))
    every = (0, 1, 2, 3)

    def backward(g, side, feature, places):
        span = pl.ds(g * thin, thin)
        left = jnp.concatenate([group[g, partners[q] * 2 + side, :, feature] for q in every], axis=0)
        right = jnp.concatenate([dense[partners[q] * 2 + side, span, places] for q in every], axis=0)
        return lax.dot_general(left, right, turn, preferred_element_type=F32)

    def crossed(g):
        for q in every:
            over(g, q, 1 - x).wait_recv()

    def weight_sum(stage):
        for copy in stages[stage - 1]:
            copy.wait_recv()
        if stage == 1:
            total = w1send[r].astype(F32)
            for k in range(1, n_row):
                total += w1recv[k].astype(F32)
            w2[...] = total.reshape(w2.shape)
            w2send[...] = w2[1 - x].astype(BF16)
            stages.append([send(w2send, w2recv, r, xpeer)])
        elif stage == 2:
            w3[z] = (w2[x] + w2recv[...].astype(F32)).astype(BF16)
            stages.append([send(w3.at[z], w3.at[z], r, (c + 2 * k) % n_col) for k in range(1, n_z)])
        elif stage == 3:
            total = w3[0].astype(F32)
            for k in range(1, n_z):
                total += w3[k].astype(F32)
            whole[r, x] = (total * scale).astype(BF16)
            mine = whole.at[r, x]
            stages.append([send(mine, mine, (r + k) % n_row, c) for k in range(1, n_row)])
            stages[-1].append(send(mine, mine, r, xpeer))
            stages[-1] += [send(mine, mine, (r + k) % n_row, xpeer) for k in range(1, n_row)]

    full = slice(None)
    for h in range(PIECES):
        reduce_pair(h)
    for h in range(PIECES):
        settle(h)
    term = lax.dot_general(aggs[...], dpres[...], turn, preferred_element_type=F32)
    part = term.shape[0] // n_row
    for k in range(n_row):
        w1send[k] = term[k * part : (k + 1) * part].astype(BF16)
    stages = [
        [send(w1send.at[(r + k) % n_row], w1recv.at[k], (r + k) % n_row, c) for k in range(1, n_row)]
    ]
    for g in range(PIECES - 1):
        take(g, 1)
        inner_take((3, g), (2, g))
    outer_take((2, 0), (3, 0))
    take(3, 1)
    inner_take((3, 3), (2, 3))
    weight_sum(1)
    outer_take((2, 1), (3, 1), (3, 3), (2, 3), (2, 2), (3, 2))
    for g in range(PIECES):
        back[...] = (back[...] if g else 0.0) + backward(g, x, full, full)
    for g in range(PIECES - 1):
        crossed(g)
        back[...] += backward(g, 1 - x, full, full)
    weight_sum(2)
    crossed(3)

    def place(p):
        return pl.ds(p * block, block)

    seconds, lasts = [], []
    spans = [pl.ds(f * half, half) for f in range(2)]
    for rows_f in spans:
        bsend[1, rows_f] = back[rows_f, place(3)] + backward(3, 1 - x, rows_f, place(3))
        seconds.append(send(bsend.at[1, rows_f], brecv.at[1, rows_f], core, c))
    ahead = back[:, place(2)] + backward(3, 1 - x, full, place(2))
    for f, rows_f in enumerate(spans):
        seconds[f].wait_recv()
        ysend[rows_f] = (ahead[f * half : (f + 1) * half] + brecv[1, rows_f]).astype(BF16)
        lasts.append(send(ysend.at[rows_f], yrecv.at[rows_f], across, c))
    bsend[0] = back[:, place(1)] + backward(3, 1 - x, full, place(1))
    first = send(bsend.at[0], brecv.at[0], core, c)
    total = back[:, place(0)] + backward(3, 1 - x, full, place(0))
    first.wait_recv()
    total += brecv[0]
    weight_sum(3)
    for copy in lasts:
        copy.wait_recv()
    total += yrecv[...].astype(F32)
    gf[...] = total.T.astype(BF16)
    weight_sum(4)
    gw[...] = whole[...].astype(F32).reshape(gw.shape)
    for copy in started:
        copy.wait_send()
    for g in range(PIECES):
        for q in range(n_z):
            over(g, q, x).wait_send()
        if g < PIECES - 1:
            near(g).wait_send()
            far(g).wait_send()

            @pl.when(inner == 1)
            def _():
                for q in (2, 3):
                    relay(g, q).wait_send()
        else:
            for q in (3, 2, 1):
                straight(g, q).wait_send()


def finish_kernel(act, gf, gw, act_out, gf_out, gw_out, sems):
    copies = []
    for k, (src, dst) in enumerate(((act, act_out), (gf, gf_out), (gw, gw_out))):
        copies.append(pltpu.make_async_copy(src, dst, sems.at[k]))
        copies[-1].start()
    for copy in copies:
        copy.wait()


def dense_per_device(feats, weight, cotangent, tile_rows, tile_cols, counts, block_values):
    n_row = lax.axis_size("row")
    n_col = lax.axis_size("col")
    block, width = feats.shape
    dense = densify(n_col, n_row, tile_rows, tile_cols, counts, block_values[0, 0])
    scale = float(block * n_row * n_col) ** -0.5
    panel = [feats] + [
        lax.ppermute(feats, "row", [(i, i ^ k) for i in range(n_row)])
        for k in range(1, n_row)
    ]
    n_z = n_col // 2
    tile = (block, width)
    part = (width // n_row, width)
    slim = (part[0] // 2, width)
    thin = (block // PIECES, width)
    copies = PIECES * (2 * n_z - 1) + 3 * n_row - 2 + n_z + 5
    vmem = pl.BlockSpec(memory_space=pltpu.VMEM)
    shapes = (
        jax.ShapeDtypeStruct(tile, BF16),
        jax.ShapeDtypeStruct(tile, BF16),
        jax.ShapeDtypeStruct((width, width), F32),
    )
    results = pl.pallas_call(
        functools.partial(layer_kernel, n_row, n_col, scale),
        out_shape=shapes,
        in_specs=[vmem] * (n_row + 3),
        out_specs=(vmem, vmem, vmem),
        scratch_shapes=[
            pltpu.VMEM((n_col, block, n_row * block), BF16),
            pltpu.VMEM((PIECES, n_z, *thin), BF16),
            pltpu.VMEM((PIECES, n_z, *thin), BF16),
            pltpu.VMEM((PIECES, n_z, *thin), F32),
            pltpu.VMEM((PIECES, n_z, *thin), BF16),
            pltpu.VMEM((PIECES, n_z, *thin), BF16),
            pltpu.VMEM((PIECES, n_col, *thin), BF16),
            pltpu.VMEM((width, n_row * block), F32),
            pltpu.VMEM((2, *tile), F32),
            pltpu.VMEM((2, *tile), F32),
            pltpu.VMEM(tile, BF16),
            pltpu.VMEM(tile, BF16),
            pltpu.VMEM(tile, BF16),
            pltpu.VMEM(tile, BF16),
            pltpu.VMEM((width, width), BF16),
            pltpu.VMEM((n_row, *part), BF16),
            pltpu.VMEM((n_row, *part), BF16),
            pltpu.VMEM((2, *slim), F32),
            pltpu.VMEM(slim, BF16),
            pltpu.VMEM(slim, BF16),
            pltpu.VMEM((n_z, *slim), BF16),
            pltpu.VMEM((n_row, 2, *slim), BF16),
            pltpu.SemaphoreType.DMA((copies,)),
            pltpu.SemaphoreType.DMA((copies,)),
            pltpu.SemaphoreType.DMA((PIECES, n_z)),
            pltpu.SemaphoreType.DMA((PIECES, n_z)),
            pltpu.SemaphoreType.DMA((PIECES, n_z)),
            pltpu.SemaphoreType.DMA((PIECES, n_z)),
        ],
        compiler_params=pltpu.CompilerParams(
            collective_id=0, has_side_effects=True, vmem_limit_bytes=28 * 2**20
        ),
        name="layer",
    )(*panel, weight, cotangent, dense)
    return pl.pallas_call(
        finish_kernel,
        out_shape=shapes,
        in_specs=[vmem] * 3,
        out_specs=(pl.BlockSpec(memory_space=pltpu.HBM),) * 3,
        scratch_shapes=[pltpu.SemaphoreType.DMA((3,))],
        compiler_params=pltpu.CompilerParams(vmem_limit_bytes=2 * 2**20),
        name="finish",
    )(*results)


def solution(mesh):
    in_specs = (
        P(("row", "col"), None),
        P(),
        P(("row", "col"), None),
        P("row", "col", None),
        P("row", "col", None),
        P("row", "col"),
        P("row", "col", None, None, None),
    )
    out_specs = (P(("row", "col"), None), P(("row", "col"), None), P())
    grid = (mesh.shape["row"], mesh.shape["col"])
    body = dense_per_device if grid == (4, 8) else per_device
    return jax.shard_map(
        body, mesh=mesh, in_specs=in_specs, out_specs=out_specs, check_vma=False
    )
```
